32 devices in a mesh: layer: 16 (over z, y, core), dp: 2 (over x).
Axes of the slice: x: 2, y: 2, z: 4, core: 2. Of those that a mesh axis runs over, the one named last changes fastest.
Arguments:
- c_guess: float32 [16, 256, 512], P('layer', 'dp'), may hold values from -6 to 6
- adj_guess: float32 [16, 256, 512], P('layer', 'dp'), may hold values from -6 to 6
- norm_gain: float32 [32, 512], P('layer'), may hold values from 0.5 to 1.5
- w_up: bfloat16 [32, 512, 2048], P('layer'), may hold values from -0.25 to 0.25
- w_down: bfloat16 [32, 2048, 512], P('layer'), may hold values from -0.125 to 0.125
- coarse_rate: float32 [16, 512], P('layer'), may hold values from 0.5 to 1
Outputs:
- c_points: float32 [16, 256, 512], P('layer', 'dp')
- adj_points: float32 [16, 256, 512], P('layer', 'dp')
- grad_up: float32 [32, 512, 2048], P('layer', 'dp')
- grad_down: float32 [32, 2048, 512], P('layer', 'dp')
The draws below stay inside these ranges and needn't reach their ends.
All inputs are finite; a program needn't handle non-finite values.
Results may differ from the reference program's by a relative error of at most 0.018.
Values may be sent and summed in bfloat16 or wider, within the bound.
A program may use at most 64 MiB of HBM per device.

```python
import jax
import jax.numpy as jnp
from jax import lax

MODEL_WIDTH = 512
FF = 2048
LPB = 2
DEPTH = 32
TOKENS = 256
N_LAYER = 16


def draw_coarse_rate(key, part):
    root_random_key = jax.random.fold_in(key, 4711)
    gentle_rate_key, quick_rate_key, selection_key, spike_rows_key, spike_size_key = jax.random.split(root_random_key, 5)
    fraction = jax.random.uniform(gentle_rate_key, (N_LAYER, MODEL_WIDTH), jnp.float32, 0.0, 1.0)
    slow_rates = jnp.exp(jnp.log(jnp.float32(0.1)) / N_LAYER * fraction)
    fast_rates = jnp.exp(jax.random.uniform(quick_rate_key, (N_LAYER, MODEL_WIDTH), jnp.float32, jnp.log(0.5), jnp.log(0.9)))
    slow_channel = jax.random.randint(selection_key, (1, MODEL_WIDTH), 0, 2)
    rate_values = jnp.where(slow_channel == 1, slow_rates, fast_rates)
    spike_row_count = jax.random.randint(spike_rows_key, (2,), 0, N_LAYER)
    block_number = jnp.arange(N_LAYER, dtype=jnp.int32)
    spike_selected = jnp.any(block_number[:, None] == spike_row_count[None, :], axis=1)
    spike_multiplier = jax.random.uniform(spike_size_key, (N_LAYER, MODEL_WIDTH), jnp.float32, 0.55, 0.8)
    rate_values = jnp.where(spike_selected[:, None], jnp.maximum(rate_values * spike_multiplier, 0.5), rate_values)
    return jnp.clip(rate_values, 0.5, 1.0).astype(jnp.float32)


def levels(own_key, shape, shards, least, top_value):
    gain, own = 1.0, jax.random.fold_in(own_key, 6)
    for axis_at, shards_of in shards:
        steps = jnp.exp(jax.random.uniform(jax.random.fold_in(own, axis_at), (shards_of,), jnp.float32, least / len(shards), top_value / len(shards)))
        gain = gain * jnp.repeat(steps, shape[axis_at] // shards_of).reshape([-1 if axis == axis_at else 1 for axis in range(len(shape))])
    return gain


def normal_values(rng, shape, spread, reach, shards=(), held_as=jnp.bfloat16):
    loudness = levels(rng, shape, shards, -0.22, 0.18) if shards else 1.0
    entries = jax.random.normal(rng, shape, jnp.float32) * spread * loudness
    return jnp.minimum(jnp.maximum(entries, -reach), reach).astype(held_as)


def setup_inputs(seed: int = 0) -> dict:
    key_list = jax.random.split(jax.random.key(seed), 7)
    return {
        "c_guess": normal_values(key_list[0], (N_LAYER, TOKENS, MODEL_WIDTH), 1.0, 6.0, ((0, 16), (1, 2)), jnp.float32),
        "adj_guess": normal_values(key_list[1], (N_LAYER, TOKENS, MODEL_WIDTH), 1.0, 6.0, ((0, 16), (1, 2)), jnp.float32),
        "norm_gain": jnp.clip(1.0 + 0.1 * jax.random.normal(key_list[2], (DEPTH, MODEL_WIDTH), jnp.float32), 0.5, 1.5),
        "w_up": normal_values(key_list[3], (DEPTH, MODEL_WIDTH, FF), MODEL_WIDTH ** -0.5, 0.25, ((0, 16),)),
        "w_down": normal_values(key_list[4], (DEPTH, FF, MODEL_WIDTH), FF ** -0.5, 0.125, ((0, 16),)),
        "coarse_rate": draw_coarse_rate(jax.random.fold_in(key_list[6], 71), 0),
    }


eps = 1e-06
step_length = 0.5

def normalize(state):
    inverse_rms = lax.rsqrt(lax.optimization_barrier(jnp.mean(state * state, axis=-1, keepdims=True)) + eps)
    return (state * inverse_rms, inverse_rms)

def layer_forward(state, gain_row, up_matrix, down_matrix):
    unit_state, inverse_rms = normalize(state)
    normed = (unit_state * gain_row).astype(jnp.bfloat16)
    preact = jnp.dot(normed, up_matrix, preferred_element_type=jnp.float32)
    hidden = jax.nn.silu(preact).astype(jnp.bfloat16)
    return state + step_length * jnp.dot(hidden, down_matrix, preferred_element_type=jnp.float32)

def layer_backward(state, cotangent, gain_row, up_matrix, down_matrix):
    unit_state, inverse_rms = normalize(state)
    normed = (unit_state * gain_row).astype(jnp.bfloat16)
    preact = jnp.dot(normed, up_matrix, preferred_element_type=jnp.float32)
    hidden = jax.nn.silu(preact).astype(jnp.bfloat16)
    sigmoid_pre = jax.nn.sigmoid(preact)
    out_grad = (step_length * cotangent).astype(jnp.bfloat16)
    hidden_grad = jnp.dot(out_grad, down_matrix.T, preferred_element_type=jnp.float32)
    pre_grad = (hidden_grad * sigmoid_pre * (1.0 + preact * (1.0 - sigmoid_pre))).astype(jnp.bfloat16)
    normed_grad = jnp.dot(pre_grad, up_matrix.T, preferred_element_type=jnp.float32)
    unit_grad = normed_grad * gain_row
    inner = lax.optimization_barrier(jnp.mean(unit_grad * unit_state, axis=-1, keepdims=True))
    new_cotangent = cotangent + inverse_rms * (unit_grad - unit_state * inner)
    return (new_cotangent, normed, pre_grad, hidden, out_grad)

def block_forward(state, gains, ups, downs):
    for depth_index in range(gains.shape[0]):
        state = layer_forward(state, gains[depth_index], ups[depth_index], downs[depth_index])
    return state

def block_inputs(state, gains, ups, downs):
    inputs = [state]
    for depth_index in range(gains.shape[0] - 1):
        state = layer_forward(state, gains[depth_index], ups[depth_index], downs[depth_index])
        inputs.append(state)
    return inputs

def block_backward(inputs, cotangent, gains, ups, downs):
    normed_list, pre_list, hidden_list, out_list = ([], [], [], [])
    for depth_index in reversed(range(gains.shape[0])):
        cotangent, normed, pre_grad, hidden, out_grad = layer_backward(inputs[depth_index], cotangent, gains[depth_index], ups[depth_index], downs[depth_index])
        normed_list.insert(0, normed)
        pre_list.insert(0, pre_grad)
        hidden_list.insert(0, hidden)
        out_list.insert(0, out_grad)
    factors = (jnp.stack(normed_list), jnp.stack(pre_list), jnp.stack(hidden_list), jnp.stack(out_list))
    return (cotangent, factors)

def reference(c_guess, adj_guess, norm_gain, w_up, w_down, coarse_rate):
    gains = norm_gain.reshape(N_LAYER, LPB, MODEL_WIDTH)
    ups = w_up.reshape(N_LAYER, LPB, MODEL_WIDTH, FF)
    downs = w_down.reshape(N_LAYER, LPB, FF, MODEL_WIDTH)

    def relax_forward(items):
        return block_forward(items[0], items[1], items[2], items[3])
    ends = lax.map(relax_forward, (c_guess, gains, ups, downs))

    def forward_step(carry, items):
        block_end, decay, guess = items
        updated = block_end + decay * (carry - guess)
        return (updated, updated)
    _, later_points = lax.scan(forward_step, c_guess[0], (ends[:-1], coarse_rate[:-1], c_guess[:-1]))
    c_points = jnp.concatenate([c_guess[:1], later_points], axis=0)

    def relax_adjoint(items):
        point, cotangent, gain_blk, up_blk, down_blk = items
        inputs = block_inputs(point, gain_blk, up_blk, down_blk)
        begin, _ = block_backward(inputs, cotangent, gain_blk, up_blk, down_blk)
        return begin
    starts = lax.map(relax_adjoint, (c_points, adj_guess, gains, ups, downs))

    def adjoint_step(carry, items):
        begin, decay, guess = items
        updated = begin + decay * (carry - guess)
        return (updated, updated)
    _, earlier_points = lax.scan(adjoint_step, adj_guess[-1], (starts[1:], coarse_rate[1:], adj_guess[1:]), reverse=True)
    adj_points = jnp.concatenate([earlier_points, adj_guess[-1:]], axis=0)

    def gradients(items):
        point, cotangent, gain_blk, up_blk, down_blk = items
        inputs = block_inputs(point, gain_blk, up_blk, down_blk)
        _, factors = block_backward(inputs, cotangent, gain_blk, up_blk, down_blk)
        normed, pre_grad, hidden, out_grad = factors
        up_grad = jnp.einsum('ltd,ltf->ldf', normed.astype(jnp.float32), pre_grad.astype(jnp.float32))
        down_grad = jnp.einsum('ltf,ltd->lfd', hidden.astype(jnp.float32), out_grad.astype(jnp.float32))
        return (up_grad, down_grad)
    up_grads, down_grads = lax.map(gradients, (c_points, adj_points, gains, ups, downs))
    return (c_points, adj_points, up_grads.reshape(DEPTH, MODEL_WIDTH, FF), down_grads.reshape(DEPTH, FF, MODEL_WIDTH))
```

```python
import functools

import jax
import jax.numpy as jnp
from jax import lax
from jax.experimental import pallas as pl
from jax.experimental.pallas import tpu as pltpu
from jax.sharding import PartitionSpec as P

eps = 1e-06
step_length = 0.5
MESH = pl.DeviceIdType.MESH
F32 = jnp.float32
BF16 = jnp.bfloat16


def dot(a, b):
    return jnp.dot(a, b, preferred_element_type=F32)


def dot_t(a, b):
    return lax.dot_general(a, b, (((1,), (1,)), ((), ())), preferred_element_type=F32)


def unit_of(state):
    r = lax.rsqrt(jnp.mean(state * state, axis=-1, keepdims=True) + eps)
    return state * r, r


def kernel(
    n, group, tile,
    guess_ref, adj_ref, gain_ref, rate_ref, up_hbm, down_hbm,
    point_ref, adjoint_ref, normed_ref, pre_ref, hidden_ref, outg_ref,
    up, down, slope, acc, states, operand,
    rates, shift_out, shift_in, part_out, part_in, cross_out, cross_in,
    w_sem, rate_send, rate_recv, shift_send, shift_recv, part_send, part_recv,
    cross_send, cross_recv,
):
    me = lax.axis_index("layer")
    mine = lax.axis_index("dp")
    layers, width, ff = up.shape
    tokens = guess_ref.shape[0]
    share = tokens // n
    tiles = ff // tile

    barrier = pltpu.get_barrier_semaphore()

    @pl.loop(1, n)
    def _(d):
        pl.semaphore_signal(
            barrier, inc=1, device_id={"layer": lax.rem(me + d, n)}, device_id_type=MESH
        )

    for q in range(1, group):
        pl.semaphore_signal(
            barrier, inc=1, device_id={"dp": lax.rem(mine + q, group)}, device_id_type=MESH
        )

    loads = []
    for l in range(layers):
        loads.append(
            (
                pltpu.make_async_copy(up_hbm.at[l], up.at[l], w_sem.at[2 * l]),
                pltpu.make_async_copy(down_hbm.at[l], down.at[l], w_sem.at[2 * l + 1]),
            )
        )
    for a, b in loads:
        a.start()
        b.start()

    def columns(f):
        return pl.ds(pl.multiple_of(f * tile, tile), tile)

    def forward(l, state, slot, with_down, before_down=None):
        unit, _ = unit_of(state)
        normed = (unit * gain_ref[pl.ds(l, 1), :]).astype(BF16)
        operand[...] = normed
        if slot is not None:
            normed_ref[l, slot] = normed
        acc[...] = jnp.zeros_like(acc)

        @pl.loop(0, tiles)
        def _(f):
            cols = columns(f)
            preact = dot(operand[...], up[l, :, cols])
            s = 0.5 + 0.5 * jnp.tanh(0.5 * preact)
            hidden = (preact * s).astype(BF16)
            if slot is not None:
                hidden_ref[l, slot, :, cols] = hidden
                slope[l, slot, :, cols] = s * (1.0 + preact * (1.0 - s))
            if with_down:
                acc[...] += dot(hidden, down[l, cols, :])

        return state + step_length * acc[...]

    def backward(l, state, cotangent, slot, keep, with_input):
        out_grad = (step_length * cotangent).astype(BF16)
        operand[...] = out_grad
        if keep:
            outg_ref[l, slot] = out_grad
        acc[...] = jnp.zeros_like(acc)

        @pl.loop(0, tiles)
        def _(f):
            cols = columns(f)
            pre = (dot_t(operand[...], down[l, cols, :]) * slope[l, slot, :, cols]).astype(BF16)
            if keep:
                pre_ref[l, slot, :, cols] = pre
            if with_input:
                acc[...] += dot_t(pre, up[l, :, cols])

        if not with_input:
            return None
        unit, r = unit_of(state)
        unit_grad = acc[...] * gain_ref[pl.ds(l, 1), :]
        inner = jnp.mean(unit_grad * unit, axis=-1, keepdims=True)
        return cotangent + r * (unit_grad - unit * inner)

    def block_inputs(start, slot):
        states[slot, 0] = start
        state = start
        for l in range(layers):
            state = forward(l, state, slot, l < layers - 1)
            if l < layers - 1:
                states[slot, l + 1] = state

    def block_backward(cotangent, slot, keep):
        for l in reversed(range(layers)):
            cotangent = backward(
                l, states[slot, l], cotangent, slot, keep, l > 0 or not keep
            )
        return cotangent

    def exchange(src, dst, send, recv, src_at, peer):
        return pltpu.make_async_remote_copy(
            src_ref=src.at[src_at],
            dst_ref=dst.at[me],
            send_sem=send.at[peer],
            recv_sem=recv.at[me],
            device_id={"layer": peer},
            device_id_type=MESH,
        )

    def arrival(src, dst, send, recv, peer):
        return pltpu.make_async_remote_copy(
            src_ref=src.at[peer],
            dst_ref=dst.at[peer],
            send_sem=send.at[peer],
            recv_sem=recv.at[peer],
            device_id={"layer": peer},
            device_id_type=MESH,
        )

    def start_sweep(phase, shift):
        src, dst = shift_out.at[phase], shift_in.at[phase]
        for k in range(n):
            src[k] = shift[k * share : (k + 1) * share].astype(BF16)
        dst[me] = src[me]

        @pl.loop(1, n)
        def _(d):
            peer = lax.rem(me + d, n)
            exchange(src, dst, shift_send.at[phase], shift_recv.at[phase], peer, peer).start()

    def finish_sweep(phase, reverse, out):
        src, dst = shift_out.at[phase], shift_in.at[phase]
        psrc, pdst = part_out.at[phase], part_in.at[phase]

        def step(k, before):
            j = n - 1 - k if reverse else k
            psrc[j] = before.astype(BF16)

            @pl.when(j == me)
            def _():
                pdst[j] = before.astype(BF16)

            @pl.when(j != me)
            def _():
                exchange(psrc, pdst, part_send.at[phase], part_recv.at[phase], j, j).start()
                arrival(src, dst, shift_send.at[phase], shift_recv.at[phase], j).wait_recv()
                if phase == 0:
                    arrival(rates, rates, rate_send, rate_recv, j).wait_recv()

            here = dst[j].astype(F32)
            return jnp.where(k == 0, here, here + rates[j] * before)

        lax.fori_loop(0, n, step, jnp.zeros((share, width), F32))

        @pl.loop(1, n)
        def _(d):
            peer = lax.rem(me + d, n)
            arrival(psrc, pdst, part_send.at[phase], part_recv.at[phase], peer).wait_recv()

        for k in range(n):
            out[k * share : (k + 1) * share, :] = pdst[k].astype(F32)

    def cross(phase, q):
        peer = lax.rem(mine + q, group)
        return pltpu.make_async_remote_copy(
            src_ref=cross_out.at[phase],
            dst_ref=cross_in.at[phase, q - 1],
            send_sem=cross_send.at[phase, q - 1],
            recv_sem=cross_recv.at[phase, q - 1],
            device_id={"dp": peer},
            device_id_type=MESH,
        )

    rates[me] = rate_ref[...]
    guess = guess_ref[...]
    state = guess
    for l in range(layers):
        loads[l][0].wait()
        loads[l][1].wait()
        state = forward(l, state, None, True)
        if l == 0:
            pl.semaphore_wait(barrier, n - 1 + group - 1)

            @pl.loop(1, n)
            def _(d):
                peer = lax.rem(me + d, n)
                exchange(rates, rates, rate_send, rate_recv, me, peer).start()

    shift = state - jnp.where(me == 0, 0.0, 1.0) * (rate_ref[...] * guess)
    start_sweep(0, shift)
    finish_sweep(0, False, point_ref)

    @pl.when(me == 0)
    def _():
        point_ref[...] = guess_ref[...]

    cross_out[0] = point_ref[...].astype(BF16)
    for q in range(1, group):
        cross(0, q).start()

    block_inputs(point_ref[...], 0)
    begin = block_backward(adj_ref[...], 0, False)
    shift = begin - jnp.where(me == n - 1, 0.0, 1.0) * (rate_ref[...] * adj_ref[...])
    start_sweep(1, shift)
    for q in range(1, group):
        cross(0, q).wait_recv()
        block_inputs(cross_in[0, q - 1].astype(F32), q)
    finish_sweep(1, True, adjoint_ref)

    @pl.when(me == n - 1)
    def _():
        adjoint_ref[...] = adj_ref[...]

    cross_out[1] = adjoint_ref[...].astype(BF16)
    for q in range(1, group):
        cross(1, q).start()
    block_backward(adjoint_ref[...], 0, True)
    for q in range(1, group):
        cross(1, q).wait_recv()
        block_backward(cross_in[1, q - 1].astype(F32), q, True)

    for q in range(1, group):
        cross(0, q).wait_send()
        cross(1, q).wait_send()

    @pl.loop(1, n)
    def _(d):
        peer = lax.rem(me + d, n)
        arrival(rates, rates, rate_send, rate_recv, peer).wait_send()
        for phase in range(2):
            arrival(
                shift_out.at[phase], shift_in.at[phase],
                shift_send.at[phase], shift_recv.at[phase], peer,
            ).wait_send()
            arrival(
                part_out.at[phase], part_in.at[phase],
                part_send.at[phase], part_recv.at[phase], peer,
            ).wait_send()


def relax(c_guess, adj_guess, gain, rate, ups, downs):
    n, group = lax.axis_size("layer"), lax.axis_size("dp")
    tokens, width = c_guess.shape
    layers, _, ff = ups.shape
    tile = min(ff, 512)
    share = tokens // n
    vmem = pl.BlockSpec(memory_space=pltpu.VMEM)
    hbm = pl.BlockSpec(memory_space=pl.ANY)
    dma = pltpu.SemaphoreType.DMA
    return pl.pallas_call(
        functools.partial(kernel, n, group, tile),
        out_shape=(
            jax.ShapeDtypeStruct((tokens, width), F32),
            jax.ShapeDtypeStruct((tokens, width), F32),
            jax.ShapeDtypeStruct((layers, group, tokens, width), BF16),
            jax.ShapeDtypeStruct((layers, group, tokens, ff), BF16),
            jax.ShapeDtypeStruct((layers, group, tokens, ff), BF16),
            jax.ShapeDtypeStruct((layers, group, tokens, width), BF16),
        ),
        in_specs=[vmem, vmem, vmem, vmem, hbm, hbm],
        out_specs=(vmem,) * 6,
        scratch_shapes=[
            pltpu.VMEM((layers, width, ff), BF16),
            pltpu.VMEM((layers, ff, width), BF16),
            pltpu.VMEM((layers, group, tokens, ff), F32),
            pltpu.VMEM((tokens, width), F32),
            pltpu.VMEM((group, layers, tokens, width), F32),
            pltpu.VMEM((tokens, width), BF16),
            pltpu.VMEM((n, 1, width), F32),
            pltpu.VMEM((2, n, share, width), BF16),
            pltpu.VMEM((2, n, share, width), BF16),
            pltpu.VMEM((2, n, share, width), BF16),
            pltpu.VMEM((2, n, share, width), BF16),
            pltpu.VMEM((2, tokens, width), BF16),
            pltpu.VMEM((2, max(group - 1, 1), tokens, width), BF16),
            dma((2 * layers,)),
            dma((n,)), dma((n,)),
            dma((2, n)), dma((2, n)),
            dma((2, n)), dma((2, n)),
            dma((2, max(group - 1, 1))), dma((2, max(group - 1, 1))),
        ],
        compiler_params=pltpu.CompilerParams(
            collective_id=0, has_side_effects=True, vmem_limit_bytes=60 * 2**20
        ),
    )(c_guess, adj_guess, gain, rate, ups, downs)


def shards(c_guess, adj_guess, norm_gain, w_up, w_down, coarse_rate):
    group = lax.axis_size("dp")
    member = lax.axis_index("dp")
    point, adjoint, normed, pre, hidden, outg = relax(
        c_guess[0], adj_guess[0], norm_gain, coarse_rate, w_up, w_down
    )
    flat = lambda x: x.reshape(x.shape[0], -1, x.shape[-1])
    normed, pre, hidden, outg = map(flat, (normed, pre, hidden, outg))
    width_share = w_up.shape[1] // group
    hidden_share = w_up.shape[2] // group
    normed_cols = lax.dynamic_slice_in_dim(normed, member * width_share, width_share, 2)
    hidden_cols = lax.dynamic_slice_in_dim(hidden, member * hidden_share, hidden_share, 2)
    up_part = jnp.einsum("ltd,ltf->ldf", normed_cols, pre, preferred_element_type=F32)
    down_part = jnp.einsum("ltf,ltd->lfd", hidden_cols, outg, preferred_element_type=F32)
    return (point[None], adjoint[None], up_part, down_part)


def solution(mesh):
    return jax.shard_map(
        shards,
        mesh=mesh,
        in_specs=(
            P("layer", "dp", None),
            P("layer", "dp", None),
            P("layer", None),
            P("layer", None, None),
            P("layer", None, None),
            P("layer", None),
        ),
        out_specs=(
            P("layer", "dp", None),
            P("layer", "dp", None),
            P("layer", "dp", None),
            P("layer", "dp", None),
        ),
        check_vma=False,
    )
```

```python
import functools

import jax
import jax.numpy as jnp
from jax import lax
from jax.experimental import pallas as pl
from jax.experimental.pallas import tpu as pltpu
from jax.sharding import PartitionSpec as P

eps = 1e-06
step_length = 0.5
MESH = pl.DeviceIdType.MESH
F32 = jnp.float32
BF16 = jnp.bfloat16


def dot(a, b):
    return jnp.dot(a, b, preferred_element_type=F32)


def dot_t(a, b):
    return lax.dot_general(a, b, (((1,), (1,)), ((), ())), preferred_element_type=F32)


def unit_of(state):
    r = lax.rsqrt(jnp.mean(state * state, axis=-1, keepdims=True) + eps)
    return state * r, r


def kernel(
    n, group, tile, sliced,
    guess_ref, adj_ref, gain_ref, rate_ref, up_hbm, down_hbm,
    point_out, adjoint_out, normed_out, pre_out, hidden_out, outg_out,
    point_ref, adjoint_ref, normed_ref, pre_ref, hidden_ref, outg_ref,
    up, down, slope, acc, states, operand,
    rates, shift_out, shift_in, part_out, part_in, cross_out, cross_in, staged,
    w_sem, rate_send, rate_recv, shift_send, shift_recv, part_send, part_recv,
    cross_send, cross_recv, end_sem, in_sem, back_sem,
):
    me = lax.axis_index("layer")
    mine = lax.axis_index("dp")
    layers, width, ff = up.shape
    tokens = guess_ref.shape[0]
    share = tokens // n
    tiles = ff // tile
    wcols = width // group
    per = max(tiles // group, 1)
    ends = []

    def put(src, dst, sem):
        copy = pltpu.make_async_copy(src, dst, sem)
        copy.start()
        ends.append(copy)

    cross_out[0] = guess_ref[...].astype(BF16).reshape(n, share, width)
    cross_out[1] = adj_ref[...].astype(BF16).reshape(n, share, width)

    barrier = pltpu.get_barrier_semaphore()

    @pl.loop(1, n)
    def _(d):
        pl.semaphore_signal(
            barrier, inc=1, device_id={"layer": lax.rem(me + d, n)}, device_id_type=MESH
        )

    for q in range(1, group):
        pl.semaphore_signal(
            barrier, inc=1, device_id={"dp": lax.rem(mine + q, group)}, device_id_type=MESH
        )

    loads = []
    for l in range(layers):
        loads.append(
            (
                pltpu.make_async_copy(up_hbm.at[l], up.at[l], w_sem.at[2 * l]),
                pltpu.make_async_copy(down_hbm.at[l], down.at[l], w_sem.at[2 * l + 1]),
            )
        )
    for a, b in loads:
        a.start()
        b.start()

    def columns(f):
        return pl.ds(pl.multiple_of(f * tile, tile), tile)

    def forward(l, state, slot, with_down, before_down=None):
        unit, _ = unit_of(state)
        normed = (unit * gain_ref[pl.ds(l, 1), :]).astype(BF16)
        operand[...] = normed
        if slot is not None:
            if sliced:
                normed_ref[l, slot] = operand[:, pl.ds(pl.multiple_of(mine * wcols, 128), wcols)]
            else:
                normed_ref[l, slot] = normed
        acc[...] = jnp.zeros_like(acc)

        @pl.loop(0, tiles)
        def _(f):
            cols = columns(f)
            preact = dot(operand[...], up[l, :, cols])
            s = 0.5 + 0.5 * jnp.tanh(0.5 * preact)
            hidden = (preact * s).astype(BF16)
            if slot is not None:
                if sliced:
                    @pl.when(lax.div(f, per) == mine)
                    def _():
                        hidden_ref[l, slot, :, columns(lax.rem(f, per))] = hidden
                else:
                    hidden_ref[l, slot, :, cols] = hidden
                slope[l, slot, :, cols] = s * (1.0 + preact * (1.0 - s))
            if with_down:
                acc[...] += dot(hidden, down[l, cols, :])

        return state + step_length * acc[...]

    def backward(l, state, cotangent, slot, keep, with_input):
        out_grad = (step_length * cotangent).astype(BF16)
        operand[...] = out_grad
        if keep:
            outg_ref[l, slot] = out_grad
        acc[...] = jnp.zeros_like(acc)

        @pl.loop(0, tiles)
        def _(f):
            cols = columns(f)
            pre = (dot_t(operand[...], down[l, cols, :]) * slope[l, slot, :, cols]).astype(BF16)
            if keep:
                pre_ref[l, slot, :, cols] = pre
            if with_input:
                acc[...] += dot_t(pre, up[l, :, cols])

        if not with_input:
            return None
        unit, r = unit_of(state)
        unit_grad = acc[...] * gain_ref[pl.ds(l, 1), :]
        inner = jnp.mean(unit_grad * unit, axis=-1, keepdims=True)
        return cotangent + r * (unit_grad - unit * inner)

    def block_inputs(start, slot):
        states[slot, 0] = start
        state = start
        for l in range(layers):
            state = forward(l, state, slot, l < layers - 1)
            if l < layers - 1:
                states[slot, l + 1] = state
        put(normed_ref.at[:, slot], normed_out.at[:, slot], in_sem.at[slot, 0])
        put(hidden_ref.at[:, slot], hidden_out.at[:, slot], in_sem.at[slot, 1])

    def block_backward(cotangent, slot, keep):
        for l in reversed(range(layers)):
            cotangent = backward(
                l, states[slot, l], cotangent, slot, keep, l > 0 or not keep
            )
            if keep:
                put(outg_ref.at[l, slot], outg_out.at[l, slot], back_sem.at[l, slot, 0])
                put(pre_ref.at[l, slot], pre_out.at[l, slot], back_sem.at[l, slot, 1])
        return cotangent

    def exchange(src, dst, send, recv, src_at, peer):
        return pltpu.make_async_remote_copy(
            src_ref=src.at[src_at],
            dst_ref=dst.at[me],
            send_sem=send.at[peer],
            recv_sem=recv.at[me],
            device_id={"layer": peer},
            device_id_type=MESH,
        )

    def arrival(src, dst, send, recv, peer):
        return pltpu.make_async_remote_copy(
            src_ref=src.at[peer],
            dst_ref=dst.at[peer],
            send_sem=send.at[peer],
            recv_sem=recv.at[peer],
            device_id={"layer": peer},
            device_id_type=MESH,
        )

    def start_sweep(phase, shift):
        src, dst = shift_out.at[phase], shift_in.at[phase]
        for k in range(n):
            src[k] = shift[k * share : (k + 1) * share].astype(BF16)
        dst[me] = src[me]

        @pl.loop(1, n)
        def _(d):
            peer = lax.rem(me + d, n)
            exchange(src, dst, shift_send.at[phase], shift_recv.at[phase], peer, peer).start()

    def finish_sweep(phase, reverse, out):
        src, dst = shift_out.at[phase], shift_in.at[phase]
        psrc, pdst = part_out.at[phase], part_in.at[phase]

        def step(k, before):
            j = n - 1 - k if reverse else k
            psrc[j] = before.astype(BF16)

            @pl.when(j == me)
            def _():
                pdst[j] = before.astype(BF16)

            @pl.when(j != me)
            def _():
                exchange(psrc, pdst, part_send.at[phase], part_recv.at[phase], j, j).start()
                arrival(src, dst, shift_send.at[phase], shift_recv.at[phase], j).wait_recv()
                if phase == 0:
                    arrival(rates, rates, rate_send, rate_recv, j).wait_recv()

            here = dst[j].astype(F32)
            return jnp.where(k == 0, here, here + rates[j] * before)

        lax.fori_loop(0, n, step, jnp.zeros((share, width), F32))

        edge = n - 1 if reverse else 0

        def pass_on(k):
            @pl.when(me == edge)
            def _():
                for q in range(1, group):
                    cross(phase, q, cross_out.at[phase], k).start()

            @pl.when(me != edge)
            def _():
                for q in range(1, group):
                    cross(phase, q, pdst, k).start()

        pass_on(me)

        @pl.loop(1, n)
        def _(d):
            peer = lax.rem(me + d, n)
            arrival(psrc, pdst, part_send.at[phase], part_recv.at[phase], peer).wait_recv()
            pass_on(peer)

        for k in range(n):
            out[k * share : (k + 1) * share, :] = pdst[k].astype(F32)

    def cross(phase, q, src, k):
        peer = lax.rem(mine + q, group)
        return pltpu.make_async_remote_copy(
            src_ref=src.at[k],
            dst_ref=cross_in.at[phase, q - 1, k],
            send_sem=cross_send.at[phase, q - 1, k],
            recv_sem=cross_recv.at[phase, q - 1, k],
            device_id={"dp": peer},
            device_id_type=MESH,
        )

    def crossed(phase, q):
        @pl.loop(0, n)
        def _(k):
            cross(phase, q, cross_out.at[phase], k).wait_recv()

        for k in range(n):
            staged[k * share : (k + 1) * share, :] = cross_in[phase, q - 1, k].astype(F32)
        return staged[...]

    rates[me] = rate_ref[...]
    guess = guess_ref[...]
    state = guess
    for copies in loads:
        for copy in copies:
            copy.wait()
    staged[...] = jnp.zeros_like(staged)

    @pl.when(me < n - 1)
    def _():
        state = guess
        for l in range(layers):
            state = forward(l, state, None, True)
        staged[...] = state

    pl.semaphore_wait(barrier, n - 1 + group - 1)

    @pl.loop(1, n)
    def _(d):
        peer = lax.rem(me + d, n)
        exchange(rates, rates, rate_send, rate_recv, me, peer).start()

    shift = staged[...] - jnp.where(me == 0, 0.0, 1.0) * (rate_ref[...] * guess)
    start_sweep(0, shift)
    finish_sweep(0, False, point_ref)

    @pl.when(me == 0)
    def _():
        point_ref[...] = guess_ref[...]

    put(point_ref, point_out, end_sem.at[0])
    block_inputs(point_ref[...], 0)
    begin = block_backward(adj_ref[...], 0, False)
    shift = begin - jnp.where(me == n - 1, 0.0, 1.0) * (rate_ref[...] * adj_ref[...])
    start_sweep(1, shift)
    for q in range(1, group):
        block_inputs(crossed(0, q), q)
    finish_sweep(1, True, adjoint_ref)

    @pl.when(me == n - 1)
    def _():
        adjoint_ref[...] = adj_ref[...]

    put(adjoint_ref, adjoint_out, end_sem.at[1])
    block_backward(adjoint_ref[...], 0, True)
    for q in range(1, group):
        block_backward(crossed(1, q), q, True)

    for q in range(1, group):
        @pl.loop(0, n)
        def _(k):
            for phase in range(2):
                cross(phase, q, cross_out.at[phase], k).wait_send()

    @pl.loop(1, n)
    def _(d):
        peer = lax.rem(me + d, n)
        arrival(rates, rates, rate_send, rate_recv, peer).wait_send()
        for phase in range(2):
            arrival(
                shift_out.at[phase], shift_in.at[phase],
                shift_send.at[phase], shift_recv.at[phase], peer,
            ).wait_send()
            arrival(
                part_out.at[phase], part_in.at[phase],
                part_send.at[phase], part_recv.at[phase], peer,
            ).wait_send()

    for copy in ends:
        copy.wait()


def relax(c_guess, adj_guess, gain, rate, ups, downs):
    n, group = lax.axis_size("layer"), lax.axis_size("dp")
    tokens, width = c_guess.shape
    layers, _, ff = ups.shape
    tile = min(ff, 512)
    share = tokens // n
    sliced = (width // group) % 128 == 0 and (ff // group) % tile == 0
    wcols = width // group if sliced else width
    fcols = ff // group if sliced else ff
    vmem = pl.BlockSpec(memory_space=pltpu.VMEM)
    hbm = pl.BlockSpec(memory_space=pl.ANY)
    dma = pltpu.SemaphoreType.DMA
    others = max(group - 1, 1)
    return pl.pallas_call(
        functools.partial(kernel, n, group, tile, sliced),
        out_shape=(
            jax.ShapeDtypeStruct((tokens, width), F32),
            jax.ShapeDtypeStruct((tokens, width), F32),
            jax.ShapeDtypeStruct((layers, group, tokens, wcols), BF16),
            jax.ShapeDtypeStruct((layers, group, tokens, ff), BF16),
            jax.ShapeDtypeStruct((layers, group, tokens, fcols), BF16),
            jax.ShapeDtypeStruct((layers, group, tokens, width), BF16),
        ),
        in_specs=[vmem, vmem, vmem, vmem, hbm, hbm],
        out_specs=(hbm,) * 6,
        scratch_shapes=[
            pltpu.VMEM((tokens, width), F32),
            pltpu.VMEM((tokens, width), F32),
            pltpu.VMEM((layers, group, tokens, wcols), BF16),
            pltpu.VMEM((layers, group, tokens, ff), BF16),
            pltpu.VMEM((layers, group, tokens, fcols), BF16),
            pltpu.VMEM((layers, group, tokens, width), BF16),
            pltpu.VMEM((layers, width, ff), BF16),
            pltpu.VMEM((layers, ff, width), BF16),
            pltpu.VMEM((layers, group, tokens, ff), F32),
            pltpu.VMEM((tokens, width), F32),
            pltpu.VMEM((group, layers, tokens, width), F32),
            pltpu.VMEM((tokens, width), BF16),
            pltpu.VMEM((n, 1, width), F32),
            pltpu.VMEM((2, n, share, width), BF16),
            pltpu.VMEM((2, n, share, width), BF16),
            pltpu.VMEM((2, n, share, width), BF16),
            pltpu.VMEM((2, n, share, width), BF16),
            pltpu.VMEM((2, n, share, width), BF16),
            pltpu.VMEM((2, others, n, share, width), BF16),
            pltpu.VMEM((tokens, width), F32),
            dma((2 * layers,)),
            dma((n,)), dma((n,)),
            dma((2, n)), dma((2, n)),
            dma((2, n)), dma((2, n)),
            dma((2, others, n)), dma((2, others, n)),
            dma((2,)), dma((group, 2)), dma((layers, group, 2)),
        ],
        compiler_params=pltpu.CompilerParams(
            collective_id=0, has_side_effects=True, vmem_limit_bytes=60 * 2**20
        ),
    )(c_guess, adj_guess, gain, rate, ups, downs)


def gradients_kernel(
    normed, pre, hidden, outg, point, adjoint, up_part, down_part, point_out, adjoint_out
):
    def outer(a, b):
        return lax.dot_general(a, b, (((0,), (0,)), ((), ())), preferred_element_type=F32)

    up_part[0] = outer(normed[0], pre[0])
    down_part[0] = outer(hidden[0], outg[0])
    point_out[...] = point[...]
    adjoint_out[...] = adjoint[...]


def gradients(normed, pre, hidden, outg, point, adjoint):
    layers, tokens, wcols = normed.shape
    fcols, ff, width = hidden.shape[2], pre.shape[2], outg.shape[2]
    cuts = 4 if fcols % 512 == 0 and ff % 512 == 0 else 1
    rows = point.shape[0] // (layers * cuts)
    by_layer = lambda l, f: (l, 0, 0)
    by_cut = lambda l, f: (l, 0, f)
    by_row = lambda l, f: (l * cuts + f, 0)
    return pl.pallas_call(
        gradients_kernel,
        grid=(layers, cuts),
        out_shape=(
            jax.ShapeDtypeStruct((layers, wcols, ff), F32),
            jax.ShapeDtypeStruct((layers, fcols, width), F32),
            jax.ShapeDtypeStruct(point.shape, F32),
            jax.ShapeDtypeStruct(adjoint.shape, F32),
        ),
        in_specs=[
            pl.BlockSpec((1, tokens, wcols), by_layer),
            pl.BlockSpec((1, tokens, ff // cuts), by_cut),
            pl.BlockSpec((1, tokens, fcols // cuts), by_cut),
            pl.BlockSpec((1, tokens, width), by_layer),
            pl.BlockSpec((rows, width), by_row),
            pl.BlockSpec((rows, width), by_row),
        ],
        out_specs=(
            pl.BlockSpec((1, wcols, ff // cuts), by_cut),
            pl.BlockSpec((1, fcols // cuts, width), lambda l, f: (l, f, 0)),
            pl.BlockSpec((rows, width), by_row),
            pl.BlockSpec((rows, width), by_row),
        ),
    )(normed, pre, hidden, outg, point, adjoint)


def shards(c_guess, adj_guess, norm_gain, w_up, w_down, coarse_rate):
    group = lax.axis_size("dp")
    member = lax.axis_index("dp")
    point, adjoint, normed, pre, hidden, outg = relax(
        c_guess[0], adj_guess[0], norm_gain, coarse_rate, w_up, w_down
    )
    flat = lambda x: x.reshape(x.shape[0], -1, x.shape[-1])
    normed, pre, hidden, outg = map(flat, (normed, pre, hidden, outg))
    width_share = w_up.shape[1] // group
    hidden_share = w_up.shape[2] // group
    if normed.shape[2] != width_share:
        normed = lax.dynamic_slice_in_dim(normed, member * width_share, width_share, 2)
        hidden = lax.dynamic_slice_in_dim(hidden, member * hidden_share, hidden_share, 2)
    up_part, down_part, point, adjoint = gradients(normed, pre, hidden, outg, point, adjoint)
    return (point[None], adjoint[None], up_part, down_part)


def solution(mesh):
    return jax.shard_map(
        shards,
        mesh=mesh,
        in_specs=(
            P("layer", "dp", None),
            P("layer", "dp", None),
            P("layer", None),
            P("layer", None, None),
            P("layer", None, None),
            P("layer", None),
        ),
        out_specs=(
            P("layer", "dp", None),
            P("layer", "dp", None),
            P("layer", "dp", None),
            P("layer", "dp", None),
        ),
        check_vma=False,
    )
```

```python
import functools

import jax
import jax.numpy as jnp
from jax import lax
from jax.experimental import pallas as pl
from jax.experimental.pallas import tpu as pltpu
from jax.sharding import PartitionSpec as P

eps = 1e-06
step_length = 0.5
MESH = pl.DeviceIdType.MESH
F32 = jnp.float32
BF16 = jnp.bfloat16


def dot(a, b):
    return jnp.dot(a, b, preferred_element_type=F32)


def dot_t(a, b):
    return lax.dot_general(a, b, (((1,), (1,)), ((), ())), preferred_element_type=F32)


def unit_of(state):
    r = lax.rsqrt(jnp.mean(state * state, axis=-1, keepdims=True) + eps)
    return state * r, r


def kernel(
    n, group, tile, sliced,
    guess_ref, adj_ref, gain_ref, rate_ref, up_hbm, down_hbm,
    point_out, adjoint_out, normed_out, pre_out, hidden_out, outg_out,
    point_ref, adjoint_ref, normed_ref, pre_ref, hidden_ref, outg_ref,
    up, down, slope, acc, states, operand,
    rates, shift_out, shift_in, part_out, part_in, cross_out, cross_in, staged,
    w_sem, rate_send, rate_recv, shift_send, shift_recv, part_send, part_recv,
    cross_send, cross_recv, end_sem, in_sem, back_sem,
):
    me = lax.axis_index("layer")
    mine = lax.axis_index("dp")
    layers, width, ff = up.shape
    tokens = guess_ref.shape[0]
    share = tokens // n
    tiles = ff // tile
    wcols = width // group
    per = max(tiles // group, 1)
    ends = []

    def put(src, dst, sem):
        copy = pltpu.make_async_copy(src, dst, sem)
        copy.start()
        ends.append(copy)

    cross_out[0] = guess_ref[...].astype(BF16).reshape(n, share, width)
    cross_out[1] = adj_ref[...].astype(BF16).reshape(n, share, width)

    barrier = pltpu.get_barrier_semaphore()

    @pl.loop(1, n)
    def _(d):
        pl.semaphore_signal(
            barrier, inc=1, device_id={"layer": lax.rem(me + d, n)}, device_id_type=MESH
        )

    for q in range(1, group):
        pl.semaphore_signal(
            barrier, inc=1, device_id={"dp": lax.rem(mine + q, group)}, device_id_type=MESH
        )

    loads = []
    for l in range(layers):
        loads.append(
            (
                pltpu.make_async_copy(up_hbm.at[l], up.at[l], w_sem.at[2 * l]),
                pltpu.make_async_copy(down_hbm.at[l], down.at[l], w_sem.at[2 * l + 1]),
            )
        )
    for a, b in loads:
        a.start()
        b.start()

    def columns(f):
        return pl.ds(pl.multiple_of(f * tile, tile), tile)

    def forward(l, state, slot, with_down, before_down=None):
        unit, _ = unit_of(state)
        normed = (unit * gain_ref[pl.ds(l, 1), :]).astype(BF16)
        operand[...] = normed
        if slot is not None:
            if sliced:
                normed_ref[l, slot] = operand[:, pl.ds(pl.multiple_of(mine * wcols, 128), wcols)]
            else:
                normed_ref[l, slot] = normed
        acc[...] = jnp.zeros_like(acc)

        @pl.loop(0, tiles, unroll=True)
        def _(f):
            cols = columns(f)
            preact = dot(operand[...], up[l, :, cols])
            s = 0.5 + 0.5 * jnp.tanh(0.5 * preact)
            hidden = (preact * s).astype(BF16)
            if slot is not None:
                if sliced:
                    @pl.when(lax.div(f, per) == mine)
                    def _():
                        hidden_ref[l, slot, :, columns(lax.rem(f, per))] = hidden
                else:
                    hidden_ref[l, slot, :, cols] = hidden
                slope[l, slot, :, cols] = s * (1.0 + preact * (1.0 - s))
            if with_down:
                acc[...] += dot(hidden, down[l, cols, :])

        return state + step_length * acc[...]

    def backward(l, state, cotangent, slot, keep, with_input):
        out_grad = (step_length * cotangent).astype(BF16)
        operand[...] = out_grad
        if keep:
            outg_ref[l, slot] = out_grad
        acc[...] = jnp.zeros_like(acc)

        @pl.loop(0, tiles, unroll=True)
        def _(f):
            cols = columns(f)
            pre = (dot_t(operand[...], down[l, cols, :]) * slope[l, slot, :, cols]).astype(BF16)
            if keep:
                pre_ref[l, slot, :, cols] = pre
            if with_input:
                acc[...] += dot_t(pre, up[l, :, cols])

        if not with_input:
            return None
        unit, r = unit_of(state)
        unit_grad = acc[...] * gain_ref[pl.ds(l, 1), :]
        inner = jnp.mean(unit_grad * unit, axis=-1, keepdims=True)
        return cotangent + r * (unit_grad - unit * inner)

    def block_inputs(start, slot):
        states[slot, 0] = start
        state = start
        for l in range(layers):
            state = forward(l, state, slot, l < layers - 1)
            if l < layers - 1:
                states[slot, l + 1] = state
        put(normed_ref.at[:, slot], normed_out.at[:, slot], in_sem.at[slot, 0])
        put(hidden_ref.at[:, slot], hidden_out.at[:, slot], in_sem.at[slot, 1])

    def block_backward(cotangent, slot, keep):
        for l in reversed(range(layers)):
            cotangent = backward(
                l, states[slot, l], cotangent, slot, keep, l > 0 or not keep
            )
            if keep:
                put(outg_ref.at[l, slot], outg_out.at[l, slot], back_sem.at[l, slot, 0])
                put(pre_ref.at[l, slot], pre_out.at[l, slot], back_sem.at[l, slot, 1])
        return cotangent

    def exchange(src, dst, send, recv, src_at, peer):
        return pltpu.make_async_remote_copy(
            src_ref=src.at[src_at],
            dst_ref=dst.at[me],
            send_sem=send.at[peer],
            recv_sem=recv.at[me],
            device_id={"layer": peer},
            device_id_type=MESH,
        )

    def arrival(src, dst, send, recv, peer):
        return pltpu.make_async_remote_copy(
            src_ref=src.at[peer],
            dst_ref=dst.at[peer],
            send_sem=send.at[peer],
            recv_sem=recv.at[peer],
            device_id={"layer": peer},
            device_id_type=MESH,
        )

    def start_sweep(phase, shift):
        src, dst = shift_out.at[phase], shift_in.at[phase]
        for k in range(n):
            src[k] = shift[k * share : (k + 1) * share].astype(BF16)
        dst[me] = src[me]

        @pl.loop(1, n)
        def _(d):
            peer = lax.rem(me + d, n)
            exchange(src, dst, shift_send.at[phase], shift_recv.at[phase], peer, peer).start()

    def finish_sweep(phase, reverse, out):
        src, dst = shift_out.at[phase], shift_in.at[phase]
        psrc, pdst = part_out.at[phase], part_in.at[phase]

        def step(k, before):
            j = n - 1 - k if reverse else k
            psrc[j] = before.astype(BF16)

            @pl.when(j == me)
            def _():
                pdst[j] = before.astype(BF16)

            @pl.when(j != me)
            def _():
                exchange(psrc, pdst, part_send.at[phase], part_recv.at[phase], j, j).start()
                arrival(src, dst, shift_send.at[phase], shift_recv.at[phase], j).wait_recv()
                if phase == 0:
                    arrival(rates, rates, rate_send, rate_recv, j).wait_recv()

            here = dst[j].astype(F32)
            return jnp.where(k == 0, here, here + rates[j] * before)

        lax.fori_loop(0, n, step, jnp.zeros((share, width), F32))

        edge = n - 1 if reverse else 0

        def pass_on(k):
            @pl.when(me == edge)
            def _():
                for q in range(1, group):
                    cross(phase, q, cross_out.at[phase], k).start()

            @pl.when(me != edge)
            def _():
                for q in range(1, group):
                    cross(phase, q, pdst, k).start()

        pass_on(me)

        @pl.loop(1, n)
        def _(d):
            peer = lax.rem(me + d, n)
            arrival(psrc, pdst, part_send.at[phase], part_recv.at[phase], peer).wait_recv()
            pass_on(peer)

        for k in range(n):
            out[k * share : (k + 1) * share, :] = pdst[k].astype(F32)

    def cross(phase, q, src, k):
        peer = lax.rem(mine + q, group)
        return pltpu.make_async_remote_copy(
            src_ref=src.at[k],
            dst_ref=cross_in.at[phase, q - 1, k],
            send_sem=cross_send.at[phase, q - 1, k],
            recv_sem=cross_recv.at[phase, q - 1, k],
            device_id={"dp": peer},
            device_id_type=MESH,
        )

    def crossed(phase, q):
        @pl.loop(0, n)
        def _(k):
            cross(phase, q, cross_out.at[phase], k).wait_recv()

        for k in range(n):
            staged[k * share : (k + 1) * share, :] = cross_in[phase, q - 1, k].astype(F32)
        return staged[...]

    rates[me] = rate_ref[...]
    guess = guess_ref[...]
    state = guess
    staged[...] = jnp.zeros_like(staged)

    @pl.when(me < n - 1)
    def _():
        state = guess
        for l in range(layers):
            for copy in loads[l]:
                copy.wait()
            state = forward(l, state, None, True)
        staged[...] = state

    @pl.when(me == n - 1)
    def _():
        for copies in loads:
            for copy in copies:
                copy.wait()

    pl.semaphore_wait(barrier, n - 1 + group - 1)

    @pl.loop(1, n)
    def _(d):
        peer = lax.rem(me + d, n)
        exchange(rates, rates, rate_send, rate_recv, me, peer).start()

    shift = staged[...] - jnp.where(me == 0, 0.0, 1.0) * (rate_ref[...] * guess)
    start_sweep(0, shift)
    finish_sweep(0, False, point_ref)

    @pl.when(me == 0)
    def _():
        point_ref[...] = guess_ref[...]

    put(point_ref, point_out, end_sem.at[0])
    block_inputs(point_ref[...], 0)
    begin = block_backward(adj_ref[...], 0, False)
    shift = begin - jnp.where(me == n - 1, 0.0, 1.0) * (rate_ref[...] * adj_ref[...])
    start_sweep(1, shift)
    for q in range(1, group):
        block_inputs(crossed(0, q), q)
    finish_sweep(1, True, adjoint_ref)

    @pl.when(me == n - 1)
    def _():
        adjoint_ref[...] = adj_ref[...]

    put(adjoint_ref, adjoint_out, end_sem.at[1])
    block_backward(adjoint_ref[...], 0, True)
    for q in range(1, group):
        block_backward(crossed(1, q), q, True)

    for q in range(1, group):
        @pl.loop(0, n)
        def _(k):
            for phase in range(2):
                cross(phase, q, cross_out.at[phase], k).wait_send()

    @pl.loop(1, n)
    def _(d):
        peer = lax.rem(me + d, n)
        arrival(rates, rates, rate_send, rate_recv, peer).wait_send()
        for phase in range(2):
            arrival(
                shift_out.at[phase], shift_in.at[phase],
                shift_send.at[phase], shift_recv.at[phase], peer,
            ).wait_send()
            arrival(
                part_out.at[phase], part_in.at[phase],
                part_send.at[phase], part_recv.at[phase], peer,
            ).wait_send()

    for copy in ends:
        copy.wait()


def relax(c_guess, adj_guess, gain, rate, ups, downs):
    n, group = lax.axis_size("layer"), lax.axis_size("dp")
    tokens, width = c_guess.shape
    layers, _, ff = ups.shape
    tile = min(ff, 512)
    share = tokens // n
    sliced = (width // group) % 128 == 0 and (ff // group) % tile == 0
    wcols = width // group if sliced else width
    fcols = ff // group if sliced else ff
    vmem = pl.BlockSpec(memory_space=pltpu.VMEM)
    hbm = pl.BlockSpec(memory_space=pl.ANY)
    dma = pltpu.SemaphoreType.DMA
    others = max(group - 1, 1)
    return pl.pallas_call(
        functools.partial(kernel, n, group, tile, sliced),
        out_shape=(
            jax.ShapeDtypeStruct((tokens, width), F32),
            jax.ShapeDtypeStruct((tokens, width), F32),
            jax.ShapeDtypeStruct((layers, group, tokens, wcols), BF16),
            jax.ShapeDtypeStruct((layers, group, tokens, ff), BF16),
            jax.ShapeDtypeStruct((layers, group, tokens, fcols), BF16),
            jax.ShapeDtypeStruct((layers, group, tokens, width), BF16),
        ),
        in_specs=[vmem, vmem, vmem, vmem, hbm, hbm],
        out_specs=(hbm,) * 6,
        scratch_shapes=[
            pltpu.VMEM((tokens, width), F32),
            pltpu.VMEM((tokens, width), F32),
            pltpu.VMEM((layers, group, tokens, wcols), BF16),
            pltpu.VMEM((layers, group, tokens, ff), BF16),
            pltpu.VMEM((layers, group, tokens, fcols), BF16),
            pltpu.VMEM((layers, group, tokens, width), BF16),
            pltpu.VMEM((layers, width, ff), BF16),
            pltpu.VMEM((layers, ff, width), BF16),
            pltpu.VMEM((layers, group, tokens, ff), F32),
            pltpu.VMEM((tokens, width), F32),
            pltpu.VMEM((group, layers, tokens, width), F32),
            pltpu.VMEM((tokens, width), BF16),
            pltpu.VMEM((n, 1, width), F32),
            pltpu.VMEM((2, n, share, width), BF16),
            pltpu.VMEM((2, n, share, width), BF16),
            pltpu.VMEM((2, n, share, width), BF16),
            pltpu.VMEM((2, n, share, width), BF16),
            pltpu.VMEM((2, n, share, width), BF16),
            pltpu.VMEM((2, others, n, share, width), BF16),
            pltpu.VMEM((tokens, width), F32),
            dma((2 * layers,)),
            dma((n,)), dma((n,)),
            dma((2, n)), dma((2, n)),
            dma((2, n)), dma((2, n)),
            dma((2, others, n)), dma((2, others, n)),
            dma((2,)), dma((group, 2)), dma((layers, group, 2)),
        ],
        compiler_params=pltpu.CompilerParams(
            collective_id=0, has_side_effects=True, vmem_limit_bytes=60 * 2**20
        ),
    )(c_guess, adj_guess, gain, rate, ups, downs)


def gradients_kernel(
    normed, pre, hidden, outg, point, adjoint, up_part, down_part, point_out, adjoint_out
):
    def outer(a, b):
        return lax.dot_general(a, b, (((0,), (0,)), ((), ())), preferred_element_type=F32)

    up_part[0] = outer(normed[0], pre[0])
    down_part[0] = outer(hidden[0], outg[0])
    point_out[...] = point[...]
    adjoint_out[...] = adjoint[...]


def gradients(normed, pre, hidden, outg, point, adjoint):
    layers, tokens, wcols = normed.shape
    fcols, ff, width = hidden.shape[2], pre.shape[2], outg.shape[2]
    cuts = 1 if fcols % 512 == 0 and ff % 512 == 0 else 1
    rows = point.shape[0] // (layers * cuts)
    by_layer = lambda l, f: (l, 0, 0)
    by_cut = lambda l, f: (l, 0, f)
    by_row = lambda l, f: (l * cuts + f, 0)
    return pl.pallas_call(
        gradients_kernel,
        grid=(layers, cuts),
        out_shape=(
            jax.ShapeDtypeStruct((layers, wcols, ff), F32),
            jax.ShapeDtypeStruct((layers, fcols, width), F32),
            jax.ShapeDtypeStruct(point.shape, F32),
            jax.ShapeDtypeStruct(adjoint.shape, F32),
        ),
        in_specs=[
            pl.BlockSpec((1, tokens, wcols), by_layer),
            pl.BlockSpec((1, tokens, ff // cuts), by_cut),
            pl.BlockSpec((1, tokens, fcols // cuts), by_cut),
            pl.BlockSpec((1, tokens, width), by_layer),
            pl.BlockSpec((rows, width), by_row),
            pl.BlockSpec((rows, width), by_row),
        ],
        out_specs=(
            pl.BlockSpec((1, wcols, ff // cuts), by_cut),
            pl.BlockSpec((1, fcols // cuts, width), lambda l, f: (l, f, 0)),
            pl.BlockSpec((rows, width), by_row),
            pl.BlockSpec((rows, width), by_row),
        ),
    )(normed, pre, hidden, outg, point, adjoint)


def shards(c_guess, adj_guess, norm_gain, w_up, w_down, coarse_rate):
    group = lax.axis_size("dp")
    member = lax.axis_index("dp")
    point, adjoint, normed, pre, hidden, outg = relax(
        c_guess[0], adj_guess[0], norm_gain, coarse_rate, w_up, w_down
    )
    flat = lambda x: x.reshape(x.shape[0], -1, x.shape[-1])
    normed, pre, hidden, outg = map(flat, (normed, pre, hidden, outg))
    width_share = w_up.shape[1] // group
    hidden_share = w_up.shape[2] // group
    if normed.shape[2] != width_share:
        normed = lax.dynamic_slice_in_dim(normed, member * width_share, width_share, 2)
        hidden = lax.dynamic_slice_in_dim(hidden, member * hidden_share, hidden_share, 2)
    up_part, down_part, point, adjoint = gradients(normed, pre, hidden, outg, point, adjoint)
    return (point[None], adjoint[None], up_part, down_part)


def solution(mesh):
    return jax.shard_map(
        shards,
        mesh=mesh,
        in_specs=(
            P("layer", "dp", None),
            P("layer", "dp", None),
            P("layer", None),
            P("layer", None, None),
            P("layer", None, None),
            P("layer", None),
        ),
        out_specs=(
            P("layer", "dp", None),
            P("layer", "dp", None),
            P("layer", "dp", None),
            P("layer", "dp", None),
        ),
        check_vma=False,
    )
```

```python
import functools

import jax
import jax.numpy as jnp
from jax import lax
from jax.experimental import pallas as pl
from jax.experimental.pallas import tpu as pltpu
from jax.sharding import PartitionSpec as P

eps = 1e-06
step_length = 0.5
MESH = pl.DeviceIdType.MESH
F32 = jnp.float32
BF16 = jnp.bfloat16


def dot(a, b):
    return jnp.dot(a, b, preferred_element_type=F32)


def dot_t(a, b):
    return lax.dot_general(a, b, (((1,), (1,)), ((), ())), preferred_element_type=F32)


def unit_of(state):
    r = lax.rsqrt(jnp.mean(state * state, axis=-1, keepdims=True) + eps)
    return state * r, r


def kernel(
    n, group, tile, sliced,
    guess_ref, adj_ref, gain_ref, rate_ref, up_hbm, down_hbm,
    point_out, adjoint_out, normed_out, pre_out, hidden_out, outg_out,
    point_ref, adjoint_ref, normed_ref, pre_ref, hidden_ref, outg_ref,
    up, down, slope, acc, states, operand,
    rates, shift_out, shift_in, part_out, part_in, cross_out, cross_in, staged,
    w_sem, rate_send, rate_recv, shift_send, shift_recv, part_send, part_recv,
    cross_send, cross_recv, end_sem, in_sem, back_sem,
):
    me = lax.axis_index("layer")
    mine = lax.axis_index("dp")
    layers, width, ff = up.shape
    tokens = guess_ref.shape[0]
    share = tokens // n
    tiles = ff // tile
    wcols = width // group
    per = max(tiles // group, 1)
    ends = []

    def put(src, dst, sem):
        copy = pltpu.make_async_copy(src, dst, sem)
        copy.start()
        ends.append(copy)

    cross_out[0] = guess_ref[...].astype(BF16).reshape(n, share, width)
    cross_out[1] = adj_ref[...].astype(BF16).reshape(n, share, width)

    barrier = pltpu.get_barrier_semaphore()

    @pl.loop(1, n)
    def _(d):
        pl.semaphore_signal(
            barrier, inc=1, device_id={"layer": lax.rem(me + d, n)}, device_id_type=MESH
        )

    for q in range(1, group):
        pl.semaphore_signal(
            barrier, inc=1, device_id={"dp": lax.rem(mine + q, group)}, device_id_type=MESH
        )

    loads = []
    for l in range(layers):
        loads.append(
            (
                pltpu.make_async_copy(up_hbm.at[l], up.at[l], w_sem.at[2 * l]),
                pltpu.make_async_copy(down_hbm.at[l], down.at[l], w_sem.at[2 * l + 1]),
            )
        )
    for a, b in loads:
        a.start()
        b.start()

    def columns(f):
        return pl.ds(pl.multiple_of(f * tile, tile), tile)

    def forward(l, state, slot, with_down, before_down=None):
        unit, _ = unit_of(state)
        normed = (unit * gain_ref[pl.ds(l, 1), :]).astype(BF16)
        operand[...] = normed
        if slot is not None:
            if sliced:
                normed_ref[l, slot] = operand[:, pl.ds(pl.multiple_of(mine * wcols, 128), wcols)]
            else:
                normed_ref[l, slot] = normed
        acc[...] = jnp.zeros_like(acc)

        @pl.loop(0, tiles, unroll=True)
        def _(f):
            cols = columns(f)
            preact = dot(operand[...], up[l, :, cols])
            s = 0.5 + 0.5 * jnp.tanh(0.5 * preact)
            hidden = (preact * s).astype(BF16)
            if slot is not None:
                if sliced:
                    @pl.when(lax.div(f, per) == mine)
                    def _():
                        hidden_ref[l, slot, :, columns(lax.rem(f, per))] = hidden
                else:
                    hidden_ref[l, slot, :, cols] = hidden
                slope[l, slot, :, cols] = s * (1.0 + preact * (1.0 - s))
            if with_down:
                acc[...] += dot(hidden, down[l, cols, :])

        return state + step_length * acc[...]

    def backward(l, state, cotangent, slot, keep, with_input):
        out_grad = (step_length * cotangent).astype(BF16)
        operand[...] = out_grad
        if keep:
            outg_ref[l, slot] = out_grad
        acc[...] = jnp.zeros_like(acc)

        @pl.loop(0, tiles, unroll=True)
        def _(f):
            cols = columns(f)
            pre = (dot_t(operand[...], down[l, cols, :]) * slope[l, slot, :, cols]).astype(BF16)
            if keep:
                pre_ref[l, slot, :, cols] = pre
            if with_input:
                acc[...] += dot_t(pre, up[l, :, cols])

        if not with_input:
            return None
        unit, r = unit_of(state)
        unit_grad = acc[...] * gain_ref[pl.ds(l, 1), :]
        inner = jnp.mean(unit_grad * unit, axis=-1, keepdims=True)
        return cotangent + r * (unit_grad - unit * inner)

    def block_inputs(start, slot):
        states[slot, 0] = start
        state = start
        for l in range(layers):
            state = forward(l, state, slot, l < layers - 1)
            if l < layers - 1:
                states[slot, l + 1] = state
        put(normed_ref.at[:, slot], normed_out.at[:, slot], in_sem.at[slot, 0])
        put(hidden_ref.at[:, slot], hidden_out.at[:, slot], in_sem.at[slot, 1])

    def block_backward(cotangent, slot, keep):
        for l in reversed(range(layers)):
            cotangent = backward(
                l, states[slot, l], cotangent, slot, keep, l > 0 or not keep
            )
            if keep:
                put(outg_ref.at[l, slot], outg_out.at[l, slot], back_sem.at[l, slot, 0])
                put(pre_ref.at[l, slot], pre_out.at[l, slot], back_sem.at[l, slot, 1])
        return cotangent

    def exchange(src, dst, send, recv, src_at, peer):
        return pltpu.make_async_remote_copy(
            src_ref=src.at[src_at],
            dst_ref=dst.at[me],
            send_sem=send.at[peer],
            recv_sem=recv.at[me],
            device_id={"layer": peer},
            device_id_type=MESH,
        )

    def arrival(src, dst, send, recv, peer):
        return pltpu.make_async_remote_copy(
            src_ref=src.at[peer],
            dst_ref=dst.at[peer],
            send_sem=send.at[peer],
            recv_sem=recv.at[peer],
            device_id={"layer": peer},
            device_id_type=MESH,
        )

    def start_sweep(phase, shift):
        src, dst = shift_out.at[phase], shift_in.at[phase]
        for k in range(n):
            src[k] = shift[k * share : (k + 1) * share].astype(BF16)
        dst[me] = src[me]

        @pl.loop(1, n)
        def _(d):
            peer = lax.rem(me + d, n)
            exchange(src, dst, shift_send.at[phase], shift_recv.at[phase], peer, peer).start()

    def finish_sweep(phase, reverse, out):
        src, dst = shift_out.at[phase], shift_in.at[phase]
        psrc, pdst = part_out.at[phase], part_in.at[phase]

        def step(k, before):
            j = n - 1 - k if reverse else k
            psrc[j] = before.astype(BF16)

            @pl.when(j == me)
            def _():
                pdst[j] = before.astype(BF16)

            @pl.when(j != me)
            def _():
                exchange(psrc, pdst, part_send.at[phase], part_recv.at[phase], j, j).start()
                arrival(src, dst, shift_send.at[phase], shift_recv.at[phase], j).wait_recv()
                if phase == 0:
                    arrival(rates, rates, rate_send, rate_recv, j).wait_recv()

            here = dst[j].astype(F32)
            return jnp.where(k == 0, here, here + rates[j] * before)

        lax.fori_loop(0, n, step, jnp.zeros((share, width), F32))

        edge = n - 1 if reverse else 0

        def pass_on(k):
            @pl.when(me == edge)
            def _():
                for q in range(1, group):
                    cross(phase, q, cross_out.at[phase], k).start()

            @pl.when(me != edge)
            def _():
                for q in range(1, group):
                    cross(phase, q, pdst, k).start()

        pass_on(me)

        @pl.loop(1, n)
        def _(d):
            peer = lax.rem(me + d, n)
            arrival(psrc, pdst, part_send.at[phase], part_recv.at[phase], peer).wait_recv()
            pass_on(peer)

        for k in range(n):
            out[k * share : (k + 1) * share, :] = pdst[k].astype(F32)

    def cross(phase, q, src, k):
        peer = lax.rem(mine + q, group)
        return pltpu.make_async_remote_copy(
            src_ref=src.at[k],
            dst_ref=cross_in.at[phase, q - 1, k],
            send_sem=cross_send.at[phase, q - 1, k],
            recv_sem=cross_recv.at[phase, q - 1, k],
            device_id={"dp": peer},
            device_id_type=MESH,
        )

    def crossed(phase, q):
        @pl.loop(0, n)
        def _(k):
            cross(phase, q, cross_out.at[phase], k).wait_recv()

        for k in range(n):
            staged[k * share : (k + 1) * share, :] = cross_in[phase, q - 1, k].astype(F32)
        return staged[...]

    rates[me] = rate_ref[...]
    guess = guess_ref[...]
    state = guess
    staged[...] = jnp.zeros_like(staged)

    @pl.when(me < n - 1)
    def _():
        state = guess
        for l in range(layers):
            for copy in loads[l]:
                copy.wait()
            state = forward(l, state, None, True)
        staged[...] = state

    @pl.when(me == n - 1)
    def _():
        for copies in loads:
            for copy in copies:
                copy.wait()

    pl.semaphore_wait(barrier, n - 1 + group - 1)

    @pl.loop(1, n)
    def _(d):
        peer = lax.rem(me + d, n)
        exchange(rates, rates, rate_send, rate_recv, me, peer).start()

    shift = staged[...] - jnp.where(me == 0, 0.0, 1.0) * (rate_ref[...] * guess)
    start_sweep(0, shift)
    finish_sweep(0, False, point_ref)

    @pl.when(me == 0)
    def _():
        point_ref[...] = guess_ref[...]

    put(point_ref, point_out, end_sem.at[0])
    block_inputs(point_ref[...], 0)
    begin = block_backward(adj_ref[...], 0, False)
    shift = begin - jnp.where(me == n - 1, 0.0, 1.0) * (rate_ref[...] * adj_ref[...])
    start_sweep(1, shift)
    for q in range(1, group):
        block_inputs(crossed(0, q), q)
    finish_sweep(1, True, adjoint_ref)

    @pl.when(me == n - 1)
    def _():
        adjoint_ref[...] = adj_ref[...]

    put(adjoint_ref, adjoint_out, end_sem.at[1])
    block_backward(adjoint_ref[...], 0, True)
    for q in range(1, group):
        block_backward(crossed(1, q), q, True)

    for q in range(1, group):
        @pl.loop(0, n)
        def _(k):
            for phase in range(2):
                cross(phase, q, cross_out.at[phase], k).wait_send()

    @pl.loop(1, n)
    def _(d):
        peer = lax.rem(me + d, n)
        arrival(rates, rates, rate_send, rate_recv, peer).wait_send()
        for phase in range(2):
            arrival(
                shift_out.at[phase], shift_in.at[phase],
                shift_send.at[phase], shift_recv.at[phase], peer,
            ).wait_send()
            arrival(
                part_out.at[phase], part_in.at[phase],
                part_send.at[phase], part_recv.at[phase], peer,
            ).wait_send()

    for copy in ends:
        copy.wait()


def relax(c_guess, adj_guess, gain, rate, ups, downs):
    n, group = lax.axis_size("layer"), lax.axis_size("dp")
    tokens, width = c_guess.shape
    layers, _, ff = ups.shape
    tile = min(ff, 1024)
    share = tokens // n
    sliced = (width // group) % 128 == 0 and (ff // group) % tile == 0
    wcols = width // group if sliced else width
    fcols = ff // group if sliced else ff
    vmem = pl.BlockSpec(memory_space=pltpu.VMEM)
    hbm = pl.BlockSpec(memory_space=pl.ANY)
    dma = pltpu.SemaphoreType.DMA
    others = max(group - 1, 1)
    return pl.pallas_call(
        functools.partial(kernel, n, group, tile, sliced),
        out_shape=(
            jax.ShapeDtypeStruct((tokens, width), F32),
            jax.ShapeDtypeStruct((tokens, width), F32),
            jax.ShapeDtypeStruct((layers, group, tokens, wcols), BF16),
            jax.ShapeDtypeStruct((layers, group, tokens, ff), BF16),
            jax.ShapeDtypeStruct((layers, group, tokens, fcols), BF16),
            jax.ShapeDtypeStruct((layers, group, tokens, width), BF16),
        ),
        in_specs=[vmem, vmem, vmem, vmem, hbm, hbm],
        out_specs=(hbm,) * 6,
        scratch_shapes=[
            pltpu.VMEM((tokens, width), F32),
            pltpu.VMEM((tokens, width), F32),
            pltpu.VMEM((layers, group, tokens, wcols), BF16),
            pltpu.VMEM((layers, group, tokens, ff), BF16),
            pltpu.VMEM((layers, group, tokens, fcols), BF16),
            pltpu.VMEM((layers, group, tokens, width), BF16),
            pltpu.VMEM((layers, width, ff), BF16),
            pltpu.VMEM((layers, ff, width), BF16),
            pltpu.VMEM((layers, group, tokens, ff), F32),
            pltpu.VMEM((tokens, width), F32),
            pltpu.VMEM((group, layers, tokens, width), F32),
            pltpu.VMEM((tokens, width), BF16),
            pltpu.VMEM((n, 1, width), F32),
            pltpu.VMEM((2, n, share, width), BF16),
            pltpu.VMEM((2, n, share, width), BF16),
            pltpu.VMEM((2, n, share, width), BF16),
            pltpu.VMEM((2, n, share, width), BF16),
            pltpu.VMEM((2, n, share, width), BF16),
            pltpu.VMEM((2, others, n, share, width), BF16),
            pltpu.VMEM((tokens, width), F32),
            dma((2 * layers,)),
            dma((n,)), dma((n,)),
            dma((2, n)), dma((2, n)),
            dma((2, n)), dma((2, n)),
            dma((2, others, n)), dma((2, others, n)),
            dma((2,)), dma((group, 2)), dma((layers, group, 2)),
        ],
        compiler_params=pltpu.CompilerParams(
            collective_id=0, has_side_effects=True, vmem_limit_bytes=60 * 2**20
        ),
    )(c_guess, adj_guess, gain, rate, ups, downs)


def gradients_kernel(
    normed, pre, hidden, outg, point, adjoint, up_part, down_part, point_out, adjoint_out
):
    def outer(a, b):
        return lax.dot_general(a, b, (((0,), (0,)), ((), ())), preferred_element_type=F32)

    up_part[0] = outer(normed[0], pre[0])
    down_part[0] = outer(hidden[0], outg[0])
    point_out[...] = point[...]
    adjoint_out[...] = adjoint[...]


def gradients(normed, pre, hidden, outg, point, adjoint):
    layers, tokens, wcols = normed.shape
    fcols, ff, width = hidden.shape[2], pre.shape[2], outg.shape[2]
    cuts = 1 if fcols % 512 == 0 and ff % 512 == 0 else 1
    rows = point.shape[0] // (layers * cuts)
    by_layer = lambda l, f: (l, 0, 0)
    by_cut = lambda l, f: (l, 0, f)
    by_row = lambda l, f: (l * cuts + f, 0)
    return pl.pallas_call(
        gradients_kernel,
        grid=(layers, cuts),
        out_shape=(
            jax.ShapeDtypeStruct((layers, wcols, ff), F32),
            jax.ShapeDtypeStruct((layers, fcols, width), F32),
            jax.ShapeDtypeStruct(point.shape, F32),
            jax.ShapeDtypeStruct(adjoint.shape, F32),
        ),
        in_specs=[
            pl.BlockSpec((1, tokens, wcols), by_layer),
            pl.BlockSpec((1, tokens, ff // cuts), by_cut),
            pl.BlockSpec((1, tokens, fcols // cuts), by_cut),
            pl.BlockSpec((1, tokens, width), by_layer),
            pl.BlockSpec((rows, width), by_row),
            pl.BlockSpec((rows, width), by_row),
        ],
        out_specs=(
            pl.BlockSpec((1, wcols, ff // cuts), by_cut),
            pl.BlockSpec((1, fcols // cuts, width), lambda l, f: (l, f, 0)),
            pl.BlockSpec((rows, width), by_row),
            pl.BlockSpec((rows, width), by_row),
        ),
    )(normed, pre, hidden, outg, point, adjoint)


def shards(c_guess, adj_guess, norm_gain, w_up, w_down, coarse_rate):
    group = lax.axis_size("dp")
    member = lax.axis_index("dp")
    point, adjoint, normed, pre, hidden, outg = relax(
        c_guess[0], adj_guess[0], norm_gain, coarse_rate, w_up, w_down
    )
    flat = lambda x: x.reshape(x.shape[0], -1, x.shape[-1])
    normed, pre, hidden, outg = map(flat, (normed, pre, hidden, outg))
    width_share = w_up.shape[1] // group
    hidden_share = w_up.shape[2] // group
    if normed.shape[2] != width_share:
        normed = lax.dynamic_slice_in_dim(normed, member * width_share, width_share, 2)
        hidden = lax.dynamic_slice_in_dim(hidden, member * hidden_share, hidden_share, 2)
    up_part, down_part, point, adjoint = gradients(normed, pre, hidden, outg, point, adjoint)
    return (point[None], adjoint[None], up_part, down_part)


def solution(mesh):
    return jax.shard_map(
        shards,
        mesh=mesh,
        in_specs=(
            P("layer", "dp", None),
            P("layer", "dp", None),
            P("layer", None),
            P("layer", None, None),
            P("layer", None, None),
            P("layer", None),
        ),
        out_specs=(
            P("layer", "dp", None),
            P("layer", "dp", None),
            P("layer", "dp", None),
            P("layer", "dp", None),
        ),
        check_vma=False,
    )
```
